128 devices in a mesh: expert: 8 (over y, core), row: 16 (over x, z).
Axes of the slice: x: 4, y: 4, z: 4, core: 2. Of those that a mesh axis runs over, the one named last changes fastest.
Arguments:
- sampled: int32 [8, 32], P('expert'), may hold values from 0 to 31, each once within a row
- refresh: int32 [256], P('expert'), may hold values 0 or 1
- momentum_bank: bfloat16 [256, 2048, 512], P('expert', 'row'), may hold values from -6 to 6
- weights: bfloat16 [256, 2048, 512], P('expert', 'row'), may hold values from -6 to 6
- grads: bfloat16 [256, 2048, 512], P('expert', 'row'), may hold values from -6 to 6
- basis: float32 [256, 2048, 64], P('expert', 'row'), may hold values from -0.125 to 0.125
Outputs:
- new_bank: bfloat16 [256, 2048, 512], P('expert', 'row')
- new_weights: bfloat16 [256, 2048, 512], P('expert', 'row')
The draws below stay inside these ranges and needn't reach their ends.
Inputs may be any that keep to these rules, and one draw needn't show every extreme that they name: Each row of sampled names every number of 0 to 31 once.
All inputs are finite; a program needn't handle non-finite values. No bound on the sum of `refresh` on one device may be relied on, other than what follows from the above.
Results may differ from the reference program's by a relative error of at most 0.0045.
Values may be sent and summed in bfloat16 or wider, within the bound.
No kernel may reach another device: no remote copies, remote signals or barrier semaphores. Data moves between devices by JAX's collectives and lax.ppermute only.
A program may use at most 128 MiB of HBM per device.

```python
import math
import jax
import jax.numpy as jnp
from jax import lax

D = 2048
FF = 512
RANK = 64
E_LOC = 32
ITERS = 3
S_LOC = 32
GROUPS = 8
EXPERTS = 256
SAMPLED = 256


def touch_ends(entries, rng, smallest, largest):
    place = [jax.random.randint(jax.random.fold_in(rng, axis), (), 0, length) for axis, length in enumerate(entries.shape)]
    main_axis = entries.shape.index(max(entries.shape))
    beside = place[:main_axis] + [(place[main_axis] + 1) % entries.shape[main_axis]] + place[main_axis + 1:]
    return entries.at[tuple(place)].set(smallest).at[tuple(beside)].set(largest)


def levels(rng, dims, split, low, top_value):
    factor_of, own = 1.0, jax.random.fold_in(rng, 6)
    for position, blocks in split:
        heights = jnp.exp(jax.random.uniform(jax.random.fold_in(own, position), (blocks,), jnp.float32, low / len(split), top_value / len(split)))
        factor_of = factor_of * jnp.repeat(heights, dims[position] // blocks).reshape([-1 if axis == position else 1 for axis in range(len(dims))])
    return factor_of


def normal_values(stream_key, dims, width, reach, split=(), held_as=jnp.bfloat16):
    values = jax.random.normal(stream_key, dims, jnp.float32) * width
    if len(split) > 0:
        values = levels(stream_key, dims, split, -0.22, 0.18) * values
    return jnp.clip(values, min=-reach, max=reach).astype(held_as)


def setup_inputs(seed: int = 0) -> dict:
    seeds = jax.random.split(jax.random.key(seed), 7)
    sampled = jax.vmap(lambda own: jax.random.permutation(own, E_LOC))(jax.random.split(seeds[0], GROUPS)).reshape((GROUPS, E_LOC)).astype(jnp.int32)
    refresh = touch_ends((jax.random.randint(seeds[1], (SAMPLED,), 0, 3) < 1).astype(jnp.int32), jax.random.fold_in(seeds[1], 1), 0, 1)
    momentum_bank = normal_values(seeds[2], (EXPERTS, D, FF), 1.0, 6.0, ((0, 8), (1, 16)))
    weights = normal_values(seeds[3], (SAMPLED, D, FF), 1.0, 6.0, ((0, 8), (1, 16)))
    grads = normal_values(seeds[4], (SAMPLED, D, FF), 1.0, 6.0, ((0, 8), (1, 16)))
    basis = normal_values(seeds[5], (SAMPLED, D, RANK), D ** -0.5, 0.125, ((0, 8), (1, 16)), jnp.float32)
    return {"sampled": sampled, "refresh": refresh, "momentum_bank": momentum_bank, "weights": weights, "grads": grads, "basis": basis}


momentum_decay = 0.9
residual_weight = 2.0
step_rate = 0.5
decay_rate = 0.1
coef_first = 3.4445
coef_second = -4.775
coef_third = 2.0315
epsilon = 1e-07

def newton(matrix):
    values = matrix.astype(jnp.float32)
    total_norm = jnp.sqrt(jnp.sum(values * values)) + epsilon
    iterate = (values / total_norm).astype(jnp.bfloat16)
    for sweep in range(ITERS):
        current = iterate.astype(jnp.float32)
        gram = jnp.dot(current.T, current, precision=lax.Precision.HIGHEST).astype(jnp.bfloat16)
        gram_full = lax.optimization_barrier(gram).astype(jnp.float32)
        square = jnp.dot(gram_full, gram_full, precision=lax.Precision.HIGHEST)
        poly = (coef_second * gram_full + coef_third * square).astype(jnp.bfloat16)
        poly_full = lax.optimization_barrier(poly).astype(jnp.float32)
        iterate = (coef_first * current + jnp.dot(current, poly_full, precision=lax.Precision.HIGHEST)).astype(jnp.bfloat16)
    return iterate

def reference(sampled, refresh, momentum_bank, weights, grads, basis):
    groups = sampled.shape[0]
    offsets = (jnp.arange(groups, dtype=jnp.int32) * E_LOC)[:, None]
    experts_hit = (sampled[:, :S_LOC].astype(jnp.int32) + offsets).reshape(-1).astype(jnp.int32)
    scale_step = step_rate * 0.2 * math.sqrt(max(D, FF))

    def single(items):
        index, weight_flag, weight_now, gradient, projector = items
        old = momentum_bank[index].astype(jnp.float32)
        grad_full = gradient.astype(jnp.float32)
        proj = jnp.dot(projector.T, grad_full, precision=lax.Precision.HIGHEST)
        low = jnp.dot(projector, proj, precision=lax.Precision.HIGHEST)
        mom = (momentum_decay * old + low + residual_weight * weight_flag * (grad_full - low)).astype(jnp.bfloat16)
        ortho = newton(mom)
        updated = weight_now.astype(jnp.float32) * (1.0 - step_rate * decay_rate) - scale_step * ortho.astype(jnp.float32)
        return (mom, updated.astype(jnp.bfloat16))
    moms, new_weights = lax.map(single, (experts_hit, refresh.astype(jnp.float32), weights, grads, basis))
    new_bank = momentum_bank.at[experts_hit].set(moms)
    return (new_bank, new_weights)
```

```python
import functools
import math

import jax
import jax.numpy as jnp
from jax import lax
from jax.experimental import pallas as pl
from jax.experimental.pallas import tpu as pltpu
from jax.sharding import PartitionSpec as P

D = 2048
FF = 512
HALF = 256
RANK = 64
ROWS = 128
SIDE = 4
PER_CHUNK = 16
CHUNKS = 2
PACK = ROWS + 16
FULL = PACK + RANK
MIX = SIDE * PACK + RANK
BACK = SIDE * ROWS + RANK
LAST = SIDE * ROWS + SIDE * RANK

momentum_decay = 0.9
residual_weight = 2.0
step_rate = 0.5
decay_rate = 0.1
coef_first = 3.4445
coef_second = -4.775
coef_third = 2.0315
epsilon = 1e-07


SMEM = pl.BlockSpec(memory_space=pltpu.SMEM)
VMEM = pl.BlockSpec(memory_space=pltpu.VMEM)
HBM = pl.BlockSpec(memory_space=pltpu.HBM)
bf16 = jnp.bfloat16
f32 = jnp.float32


def shape(*dims, dtype=bf16):
    return jax.ShapeDtypeStruct(dims, dtype)


def call(kernel, out_shape, in_specs, out_specs, scratch, limit, flops, moved, aliases=None):
    return pl.pallas_call(
        kernel,
        out_shape=out_shape,
        in_specs=in_specs,
        out_specs=out_specs,
        scratch_shapes=scratch,
        input_output_aliases=aliases or {},
        compiler_params=pltpu.CompilerParams(vmem_limit_bytes=limit << 20),
        cost_estimate=pl.CostEstimate(flops=int(flops), bytes_accessed=int(moved), transcendentals=0),
    )


def position():
    me = lax.axis_index("row")
    return lax.div(me, SIDE), lax.rem(me, SIDE)


def plus(place, dx, dz):
    return lax.rem(place[0] + dx, SIDE) * SIDE + lax.rem(place[1] + dz, SIDE)


def mm(a, b):
    return jnp.dot(a, b, preferred_element_type=f32)


def mm_t(a, b):
    return lax.dot_general(a, b, (((0,), (0,)), ((), ())), preferred_element_type=f32)


def halves(value):
    high = value.astype(bf16)
    return jnp.concatenate([high, (value - high.astype(f32)).astype(bf16)], axis=0)


def added(parts):
    total = parts[0].astype(f32)
    for part in parts[1:]:
        total = total + part.astype(f32)
    return total.astype(bf16)


def pack_kernel(chunk, top, chosen_in, refresh_in, grads, bank, basis, *rest):
    left, right = rest[:SIDE], rest[SIDE : 2 * SIDE]
    g, old, bt, chosen, refresh, sems, flags = rest[2 * SIDE :]
    place = position()
    base = chunk * PER_CHUNK
    small = (
        pltpu.make_async_copy(chosen_in, chosen, flags.at[0]),
        pltpu.make_async_copy(refresh_in, refresh, flags.at[1]),
    )
    for copy in small:
        copy.start()

    def copies(i):
        s = base + plus(place, i // SIDE, i % SIDE)
        return (
            pltpu.make_async_copy(grads.at[s], g.at[i], sems.at[0, i]),
            pltpu.make_async_copy(basis.at[s], bt.at[i], sems.at[1, i]),
        )

    def old_copy(i):
        s = base + plus(place, i // SIDE, i % SIDE)
        return pltpu.make_async_copy(bank.at[chosen[0, s]], old.at[i], sems.at[2, i])

    for i in range(4):
        for copy in copies(i):
            copy.start()
    for copy in small:
        copy.wait()
    for i in range(PER_CHUNK):
        if i >= 4:
            for copy in copies(i):
                copy.start()
        old_copy(i).start()

    for i in range(PER_CHUNK):
        dx, dz = i // SIDE, i % SIDE
        if dz == 0:
            for j in range(i, i + SIDE):
                for copy in copies(j):
                    copy.wait()
                old_copy(j).wait()
        flag = residual_weight * refresh[base + plus(place, dx, dz)].astype(f32)
        both = halves(bt[i])
        for side in range(2):
            cols = slice(side * HALF, (side + 1) * HALF)
            out, at = (left[dx], dz) if side == 0 else (right[dz], dx)
            at = top + at * FULL
            grad = g[i, :, cols]
            value = momentum_decay * old[i, :, cols].astype(f32) + flag * grad.astype(f32)
            out[at : at + ROWS] = value.astype(bf16)
            first = 32 * side
            out[at + ROWS : at + PACK, :128] = both[first : first + 16]
            out[at + ROWS : at + PACK, 128:] = both[first + 16 : first + 32]
            part = mm(both, grad)
            out[at + PACK : at + FULL] = (part[:RANK] + part[RANK:]).astype(bf16)


def pack(chunk, top, chosen, refresh, grads, bank, basis):
    return call(
        functools.partial(pack_kernel, chunk, top),
        [shape(top + SIDE * FULL, HALF)] * (2 * SIDE),
        [HBM] * 5,
        [VMEM] * (2 * SIDE),
        [
            pltpu.VMEM((PER_CHUNK, ROWS, FF), bf16),
            pltpu.VMEM((PER_CHUNK, ROWS, FF), bf16),
            pltpu.VMEM((PER_CHUNK, RANK, ROWS), f32),
            pltpu.SMEM((1, CHUNKS * PER_CHUNK), jnp.int32),
            pltpu.SMEM((CHUNKS * PER_CHUNK,), jnp.int32),
            pltpu.SemaphoreType.DMA((3, PER_CHUNK)),
            pltpu.SemaphoreType.DMA((2,)),
        ],
        22,
        3e8,
        9e6,
    )(chosen, refresh, grads, bank, basis)


def mix_kernel(top, count, *refs):
    outs = refs[count:]
    for side in range(2):
        got = refs[side * SIDE : (side + 1) * SIDE]
        out = outs[side * SIDE : (side + 1) * SIDE]
        for to in range(SIDE):
            at = top + to * FULL
            for src in range(SIDE):
                out[to][src * PACK : (src + 1) * PACK] = got[src][at : at + PACK]
            out[to][SIDE * PACK : MIX] = added([ref[at + PACK : at + FULL] for ref in got])


def mix(top, got, into):
    rows = MIX if into is None else into[0].shape[0]
    into = into or []
    return call(
        functools.partial(mix_kernel, top, len(got) + len(into)),
        [shape(rows, HALF)] * (2 * SIDE),
        [VMEM] * (len(got) + len(into)),
        [VMEM] * (2 * SIDE),
        [],
        16,
        1e6,
        6e6,
        {len(got) + k: k for k in range(len(into))},
    )(*got, *into)


def ortho_kernel(chunk, top, refresh, *refs):
    q_left, q_right = refs[:SIDE], refs[SIDE : 2 * SIDE]
    b_left, b_right = refs[2 * SIDE : 3 * SIDE], refs[3 * SIDE : 4 * SIDE]
    m, acc, gram, b_one, q_mat = refs[4 * SIDE :]
    place = position()
    keep = 1.0 - residual_weight * refresh[chunk * PER_CHUNK + plus(place, 0, 0)].astype(f32)
    proj = [added([ref[SIDE * PACK : MIX] for ref in q]) for q in (q_left, q_right)]
    for k in range(SIDE):
        b_left[k][top + SIDE * ROWS : top + SIDE * ROWS + RANK] = proj[0]
        b_right[k][top + SIDE * ROWS : top + SIDE * ROWS + RANK] = proj[1]

    for i in range(PER_CHUNK):
        dx, dz = i // SIDE, i % SIDE
        pieces = []
        for ref, at in ((q_left[dz], dx * PACK), (q_right[dx], dz * PACK)):
            pieces += [ref[at + ROWS : at + PACK, :128], ref[at + ROWS : at + PACK, 128:]]
        bt = jnp.concatenate(pieces, axis=0)
        for side, ref, at in ((0, q_left[dz], dx * PACK), (1, q_right[dx], dz * PACK)):
            value = ref[at : at + ROWS].astype(f32) + keep * mm_t(bt, proj[side])
            m[i * ROWS : (i + 1) * ROWS, side * HALF : (side + 1) * HALF] = value.astype(bf16)

    acc[...] = mm_t(m[:1024], m[:1024])
    acc[...] += mm_t(m[1024:], m[1024:])

    rows = lax.broadcasted_iota(jnp.int32, (FF, FF), 0)
    cols = lax.broadcasted_iota(jnp.int32, (FF, FF), 1)
    whole = acc[...]
    square_sum = jnp.sum(jnp.where(rows == cols, whole, 0.0), axis=(0, 1), keepdims=True)
    inverse = 1.0 / (jnp.sqrt(square_sum) + epsilon)
    gram[...] = ((whole * inverse) * inverse).astype(bf16)

    def factor():
        a = gram[...]
        return (coef_second * a.astype(f32) + coef_third * mm(a, a)).astype(bf16)

    def advance(b):
        a = gram[...]
        half_way = (coef_first * a.astype(f32) + mm(a, b)).astype(bf16)
        gram[...] = (coef_first * half_way.astype(f32) + mm(half_way, b)).astype(bf16)

    b_one[...] = factor()
    advance(b_one[...])
    b = factor()
    q_mat[...] = (
        coef_first * (b_one[...].astype(f32) + b.astype(f32)) + mm(b_one[...], b)
    ).astype(bf16)
    advance(b)
    b = factor()
    q = q_mat[...]
    q_mat[...] = (
        coef_first * q.astype(f32) + coef_first * coef_first * b.astype(f32) + mm(q, b)
    ).astype(bf16)

    for dx in range(SIDE):
        part = m[dx * 512 : (dx + 1) * 512, :]
        value = (inverse * (coef_first**3 * part.astype(f32) + mm(part, q_mat[...]))).astype(bf16)
        for dz in range(SIDE):
            rows = slice(dz * ROWS, (dz + 1) * ROWS)
            b_left[dz][top + dx * ROWS : top + (dx + 1) * ROWS] = value[rows, :HALF]
            b_right[dx][top + dz * ROWS : top + (dz + 1) * ROWS] = value[rows, HALF:]


def orthogonalize(chunk, top, refresh, got):
    return call(
        functools.partial(ortho_kernel, chunk, top),
        [shape(top + BACK, HALF)] * (2 * SIDE),
        [SMEM] + [VMEM] * (2 * SIDE),
        [VMEM] * (2 * SIDE),
        [
            pltpu.VMEM((D, FF), bf16),
            pltpu.VMEM((FF, FF), f32),
            pltpu.VMEM((FF, FF), bf16),
            pltpu.VMEM((FF, FF), bf16),
            pltpu.VMEM((FF, FF), bf16),
        ],
        28,
        8e9,
        5e6,
    )(refresh, *got)


def turn_kernel(top, count, *refs):
    outs = refs[count:]
    for side in range(2):
        got = refs[side * SIDE : (side + 1) * SIDE]
        out = outs[side * SIDE : (side + 1) * SIDE]
        for to in range(SIDE):
            for src in range(SIDE):
                at = top + to * ROWS
                out[to][src * ROWS : (src + 1) * ROWS] = got[src][at : at + ROWS]
                at = SIDE * ROWS + src * RANK
                out[to][at : at + RANK] = got[src][top + SIDE * ROWS : top + BACK]


def turn(top, got, into):
    rows = LAST if into is None else into[0].shape[0]
    into = into or []
    return call(
        functools.partial(turn_kernel, top, len(got) + len(into)),
        [shape(rows, HALF)] * (2 * SIDE),
        [VMEM] * (len(got) + len(into)),
        [VMEM] * (2 * SIDE),
        [],
        16,
        1e3,
        4e6,
        {len(got) + k: k for k in range(len(into))},
    )(*got, *into)


def finish_kernel(chunk, count, chosen, refresh, grads, bank, basis, weights, *refs):
    left, right = refs[:SIDE], refs[SIDE : 2 * SIDE]
    new_bank, new_weights, mom, updated, sems = refs[count:]
    place = position()
    scale_step = step_rate * 0.2 * math.sqrt(max(D, FF))
    pending = []
    for i in range(PER_CHUNK):
        dx, dz = i // SIDE, i % SIDE
        s = chunk * PER_CHUNK + plus(place, dx, dz)
        row = chosen[0, s]
        flag = residual_weight * refresh[s].astype(f32)
        both = halves(basis[s])
        for side, ref, at in ((0, left[dx], dz), (1, right[dz], dx)):
            cols = slice(side * HALF, (side + 1) * HALF)
            ortho = ref[at * ROWS : (at + 1) * ROWS].astype(f32)
            value = weights[s, :, cols].astype(f32) * (1.0 - step_rate * decay_rate) - scale_step * ortho
            updated[i, :, cols] = value.astype(bf16)
            proj = ref[SIDE * ROWS + at * RANK : SIDE * ROWS + (at + 1) * RANK]
            low = mm_t(both, jnp.concatenate([proj, proj], axis=0))
            value = (
                momentum_decay * bank[row, :, cols].astype(f32)
                + low
                + flag * (grads[s, :, cols].astype(f32) - low)
            )
            mom[i, :, cols] = value.astype(bf16)
        for copy in (
            pltpu.make_async_copy(updated.at[i], new_weights.at[s], sems.at[0, i]),
            pltpu.make_async_copy(mom.at[i], new_bank.at[row], sems.at[1, i]),
        ):
            copy.start()
            pending.append(copy)
    for copy in pending:
        copy.wait()


def finish(chunk, chosen, refresh, grads, bank, basis, weights, got, into):
    count = len(got) + len(into)
    return call(
        functools.partial(finish_kernel, chunk, count),
        [shape(CHUNKS * PER_CHUNK, ROWS, FF)] * 2,
        [SMEM] * 2 + [VMEM] * (4 + len(got)) + [HBM] * len(into),
        [HBM] * 2,
        [
            pltpu.VMEM((PER_CHUNK, ROWS, FF), bf16),
            pltpu.VMEM((PER_CHUNK, ROWS, FF), bf16),
            pltpu.SemaphoreType.DMA((2, PER_CHUNK)),
        ],
        30,
        6e8,
        1e7,
        {6 + len(got) + k: k for k in range(len(into))},
    )(chosen, refresh, grads, bank, basis, weights, *got, *into)


def send(array, dx, dz):
    pairs = [
        (x * SIDE + z, ((x + dx) % SIDE) * SIDE + (z + dz) % SIDE)
        for x in range(SIDE)
        for z in range(SIDE)
    ]
    return lax.ppermute(array, "row", pairs)


def exchange(over_x, over_z, sign):
    got_x, got_z = [over_x[0]], [over_z[0]]
    for k in (2, 1, 3):
        got_x.append(send(over_x[k], sign * k, 0))
        got_z.append(send(over_z[k], 0, sign * k))
    order = [0, 2, 1, 3]
    return [got_x[k] for k in order], [got_z[k] for k in order]


def step(sampled, refresh, bank, weights, grads, basis):
    basis_t = jnp.swapaxes(basis, 1, 2)
    state = (sampled, refresh, grads, bank, basis_t)
    kept = tuple(pltpu.with_memory_space_constraint(value, pltpu.HBM) for value in state)

    got = []
    for chunk in range(CHUNKS):
        packed = pack(chunk, 0, *kept)
        got.append(exchange(packed[:SIDE], packed[SIDE:], 1))
    arrived = []
    for chunk in range(CHUNKS):
        got_x, got_z = got[chunk]
        mixed = mix(0, got_x + got_z, None)
        got_x, got_z = exchange(mixed[SIDE:], mixed[:SIDE], 1)
        arrived.append(got_z + got_x)
    backs = [orthogonalize(0, 0, refresh, arrived[0])]
    arrived[1], _ = lax.optimization_barrier((arrived[1], backs[0][0]))
    backs.append(orthogonalize(1, 0, refresh, arrived[1]))
    outs = []
    for chunk in range(CHUNKS):
        back = backs[chunk]
        got_x, got_z = exchange(back[SIDE:], back[:SIDE], -1)
        turned = turn(0, got_z + got_x, None)
        got_x, got_z = exchange(turned[:SIDE], turned[SIDE:], -1)
        outs = list(finish(chunk, *state, weights, got_x + got_z, outs))
    return tuple(outs)


def solution(mesh):
    in_specs = (
        P("expert", None),
        P("expert"),
        P("expert", "row", None),
        P("expert", "row", None),
        P("expert", "row", None),
        P("expert", "row", None),
    )
    out_specs = (P("expert", "row", None), P("expert", "row", None))
    return jax.shard_map(step, mesh=mesh, in_specs=in_specs, out_specs=out_specs, check_vma=False)
```

```python
import functools
import math

import jax
import jax.numpy as jnp
from jax import lax
from jax.experimental import pallas as pl
from jax.experimental.pallas import tpu as pltpu
from jax.sharding import PartitionSpec as P


D = 2048
FF = 512
HALF = 256
RANK = 64
ROWS = 128
SIDE = 4
PER_CHUNK = 16
CHUNKS = 2
PACK = ROWS + 16
FULL = PACK + RANK
MIX = SIDE * PACK + RANK
BACK = SIDE * ROWS + RANK
LAST = SIDE * ROWS + SIDE * RANK

momentum_decay = 0.9
residual_weight = 2.0
step_rate = 0.5
decay_rate = 0.1
coef_first = 3.4445
coef_second = -4.775
coef_third = 2.0315
epsilon = 1e-07


SMEM = pl.BlockSpec(memory_space=pltpu.SMEM)
VMEM = pl.BlockSpec(memory_space=pltpu.VMEM)
HBM = pl.BlockSpec(memory_space=pltpu.HBM)
bf16 = jnp.bfloat16
f32 = jnp.float32


def shape(*dims, dtype=bf16):
    return jax.ShapeDtypeStruct(dims, dtype)


def call(kernel, out_shape, in_specs, out_specs, scratch, limit, flops, moved, aliases=None):
    return pl.pallas_call(
        kernel,
        out_shape=out_shape,
        in_specs=in_specs,
        out_specs=out_specs,
        scratch_shapes=scratch,
        input_output_aliases=aliases or {},
        compiler_params=pltpu.CompilerParams(vmem_limit_bytes=limit << 20),
        cost_estimate=pl.CostEstimate(flops=int(flops), bytes_accessed=int(moved), transcendentals=0),
    )


def position():
    me = lax.axis_index("row")
    return lax.div(me, SIDE), lax.rem(me, SIDE)


def plus(place, dx, dz):
    return lax.rem(place[0] + dx, SIDE) * SIDE + lax.rem(place[1] + dz, SIDE)


def mm(a, b):
    return jnp.dot(a, b, preferred_element_type=f32)


def mm_t(a, b):
    return lax.dot_general(a, b, (((0,), (0,)), ((), ())), preferred_element_type=f32)


def halves(value):
    high = value.astype(bf16)
    return jnp.concatenate([high, (value - high.astype(f32)).astype(bf16)], axis=0)


def added(parts):
    total = parts[0].astype(f32)
    for part in parts[1:]:
        total = total + part.astype(f32)
    return total.astype(bf16)


def pack_kernel(chunk, steps, chosen_in, refresh_in, grads, bank, basis, *rest):
    left, right = rest[: len(steps)], rest[len(steps) : 2 * len(steps)]
    g, old, bt, chosen, refresh, sems, flags = rest[2 * len(steps) :]
    place = position()
    base = chunk * PER_CHUNK
    small = (
        pltpu.make_async_copy(chosen_in, chosen, flags.at[0]),
        pltpu.make_async_copy(refresh_in, refresh, flags.at[1]),
    )
    for copy in small:
        copy.start()

    jobs = []
    for n, k in enumerate(steps):
        for j in range(SIDE):
            jobs.append((k * SIDE + j, 0, left[n], j))
            jobs.append((j * SIDE + k, 1, right[n], j))

    def number(i):
        return base + plus(place, i // SIDE, i % SIDE)

    def columns(side):
        return slice(side * HALF, (side + 1) * HALF)

    basis_copies = {}
    block_copies = []
    for i, side, _, _ in jobs:
        if i not in basis_copies:
            basis_copies[i] = pltpu.make_async_copy(basis.at[number(i)], bt.at[i], sems.at[2, 0, i])
            basis_copies[i].start()
        copy = pltpu.make_async_copy(
            grads.at[number(i), :, columns(side)], g.at[i, :, columns(side)], sems.at[0, side, i]
        )
        copy.start()
        block_copies.append([copy])
    for copy in small:
        copy.wait()
    for (i, side, _, _), copies in zip(jobs, block_copies):
        copy = pltpu.make_async_copy(
            bank.at[chosen[0, number(i)], :, columns(side)], old.at[i, :, columns(side)], sems.at[1, side, i]
        )
        copy.start()
        copies.append(copy)

    ready = set()
    for n, (i, side, out, at) in enumerate(jobs):
        if n % 8 == 0:
            for (later, _, _, _), copies in zip(jobs[n : n + 8], block_copies[n : n + 8]):
                for copy in copies:
                    copy.wait()
                if later not in ready:
                    basis_copies[later].wait()
                    ready.add(later)
        flag = residual_weight * refresh[number(i)].astype(f32)
        both = halves(bt[i])
        grad = g[i, :, columns(side)]
        value = momentum_decay * old[i, :, columns(side)].astype(f32) + flag * grad.astype(f32)
        at = at * FULL
        out[at : at + ROWS] = value.astype(bf16)
        first = 32 * side
        out[at + ROWS : at + PACK, :128] = both[first : first + 16]
        out[at + ROWS : at + PACK, 128:] = both[first + 16 : first + 32]
        part = mm(both, grad)
        out[at + PACK : at + FULL] = (part[:RANK] + part[RANK:]).astype(bf16)


def pack(chunk, steps, chosen, refresh, grads, bank, basis):
    outs = call(
        functools.partial(pack_kernel, chunk, steps),
        [shape(SIDE * FULL, HALF)] * (2 * len(steps)),
        [HBM] * 5,
        [VMEM] * (2 * len(steps)),
        [
            pltpu.VMEM((PER_CHUNK, ROWS, FF), bf16),
            pltpu.VMEM((PER_CHUNK, ROWS, FF), bf16),
            pltpu.VMEM((PER_CHUNK, RANK, ROWS), f32),
            pltpu.SMEM((1, CHUNKS * PER_CHUNK), jnp.int32),
            pltpu.SMEM((CHUNKS * PER_CHUNK,), jnp.int32),
            pltpu.SemaphoreType.DMA((3, 2, PER_CHUNK)),
            pltpu.SemaphoreType.DMA((2,)),
        ],
        22,
        1e8 * len(steps),
        3e6 * len(steps),
    )(chosen, refresh, grads, bank, basis)
    return dict(zip(steps, outs[: len(steps)])), dict(zip(steps, outs[len(steps) :]))


def mix_kernel(*refs):
    outs = refs[2 * SIDE :]
    for side in range(2):
        got = refs[side * SIDE : (side + 1) * SIDE]
        out = outs[side * SIDE : (side + 1) * SIDE]
        for to in range(SIDE):
            at = to * FULL
            for src in range(SIDE):
                out[to][src * PACK : (src + 1) * PACK] = got[src][at : at + PACK]
            out[to][SIDE * PACK : MIX] = added([ref[at + PACK : at + FULL] for ref in got])


def mix(got):
    return call(
        mix_kernel,
        [shape(MIX, HALF)] * (2 * SIDE),
        [VMEM] * (2 * SIDE),
        [VMEM] * (2 * SIDE),
        [],
        16,
        1e6,
        6e6,
    )(*got)


def ortho_kernel(chunk, refresh, *refs):
    q_left, q_right = refs[:SIDE], refs[SIDE : 2 * SIDE]
    b_left, b_right = refs[2 * SIDE : 3 * SIDE], refs[3 * SIDE : 4 * SIDE]
    m, acc, gram, f_one, f_two, work = refs[4 * SIDE :]
    place = position()
    keep = 1.0 - residual_weight * refresh[chunk * PER_CHUNK + plus(place, 0, 0)].astype(f32)
    proj = [added([ref[SIDE * PACK : MIX] for ref in q]) for q in (q_left, q_right)]
    near = [(keep * part.astype(f32)).astype(bf16) for part in proj]
    for k in range(SIDE):
        b_left[k][SIDE * ROWS : BACK] = proj[0]
        b_right[k][SIDE * ROWS : BACK] = proj[1]

    for i in range(PER_CHUNK):
        dx, dz = i // SIDE, i % SIDE
        pieces = []
        for ref, at in ((q_left[dz], dx * PACK), (q_right[dx], dz * PACK)):
            pieces += [ref[at + ROWS : at + PACK, :128], ref[at + ROWS : at + PACK, 128:]]
        bt = jnp.concatenate(pieces, axis=0)
        for side, ref, at in ((0, q_left[dz], dx * PACK), (1, q_right[dx], dz * PACK)):
            value = ref[at : at + ROWS].astype(f32) + mm_t(bt, near[side])
            m[i * ROWS : (i + 1) * ROWS, side * HALF : (side + 1) * HALF] = value.astype(bf16)

    acc[...] = mm_t(m[:1024], m[:1024])
    acc[...] += mm_t(m[1024:], m[1024:])

    tile = (ROWS, ROWS)
    diagonal = lax.broadcasted_iota(jnp.int32, tile, 0) == lax.broadcasted_iota(jnp.int32, tile, 1)
    blocks = [slice(k * ROWS, (k + 1) * ROWS) for k in range(FF // ROWS)]
    trace = jnp.zeros(tile, f32)
    for block in blocks:
        trace += jnp.where(diagonal, acc[block, block], 0.0)
    inverse = 1.0 / (jnp.sqrt(jnp.sum(trace, axis=(0, 1), keepdims=True)) + epsilon)
    gram[...] = (acc[...] * (inverse * inverse)).astype(bf16)

    def factor(out):
        for at in range(0, FF, HALF):
            rows = slice(at, at + HALF)
            part = gram[rows, :]
            value = coef_second * part.astype(f32) + coef_third * mm(part, gram[...])
            out[rows, :] = value.astype(bf16)
        for block in blocks:
            part = out[block, block].astype(f32)
            out[block, block] = jnp.where(diagonal, part + coef_first, part).astype(bf16)

    def advance(factor_ref):
        work[...] = mm(gram[...], factor_ref[...]).astype(bf16)
        gram[...] = mm(work[...], factor_ref[...]).astype(bf16)

    factor(f_one)
    advance(f_one)
    factor(f_two)
    advance(f_two)
    work[...] = mm(f_one[...], f_two[...]).astype(bf16)
    factor(f_one)
    f_two[...] = (inverse * mm(work[...], f_one[...])).astype(bf16)

    for dx in range(SIDE):
        value = mm(m[dx * 512 : (dx + 1) * 512, :], f_two[...]).astype(bf16)
        for dz in range(SIDE):
            rows = slice(dz * ROWS, (dz + 1) * ROWS)
            b_left[dz][dx * ROWS : (dx + 1) * ROWS] = value[rows, :HALF]
            b_right[dx][dz * ROWS : (dz + 1) * ROWS] = value[rows, HALF:]


def orthogonalize(chunk, refresh, got):
    return call(
        functools.partial(ortho_kernel, chunk),
        [shape(BACK, HALF)] * (2 * SIDE),
        [SMEM] + [VMEM] * (2 * SIDE),
        [VMEM] * (2 * SIDE),
        [
            pltpu.VMEM((D, FF), bf16),
            pltpu.VMEM((FF, FF), f32),
            pltpu.VMEM((FF, FF), bf16),
            pltpu.VMEM((FF, FF), bf16),
            pltpu.VMEM((FF, FF), bf16),
            pltpu.VMEM((FF, FF), bf16),
        ],
        28,
        8e9,
        5e6,
    )(refresh, *got)


def turn_kernel(*refs):
    outs = refs[2 * SIDE :]
    for side in range(2):
        got = refs[side * SIDE : (side + 1) * SIDE]
        out = outs[side * SIDE : (side + 1) * SIDE]
        for to in range(SIDE):
            for src in range(SIDE):
                out[to][src * ROWS : (src + 1) * ROWS] = got[src][to * ROWS : (to + 1) * ROWS]
                at = SIDE * ROWS + src * RANK
                out[to][at : at + RANK] = got[src][SIDE * ROWS : BACK]


def turn(got):
    return call(
        turn_kernel,
        [shape(LAST, HALF)] * (2 * SIDE),
        [VMEM] * (2 * SIDE),
        [VMEM] * (2 * SIDE),
        [],
        16,
        1e3,
        4e6,
    )(*got)


def finish_kernel(parts, unroll, count, chosen, refresh, grads, bank, basis, weights, *refs):
    new_bank, new_weights, mom, updated, sems = refs[count:]
    place = position()
    scale_step = step_rate * 0.2 * math.sqrt(max(D, FF))

    def blocks(n, j):
        chunk, k = parts[n]
        for side, dx, dz in ((0, k, j), (1, j, k)):
            s = chunk * PER_CHUNK + plus(place, dx, dz)
            yield side, refs[2 * n + side], n * SIDE + j, s, slice(side * HALF, (side + 1) * HALF)

    def copies(side, i, s, cols):
        return (
            pltpu.make_async_copy(updated.at[i, :, cols], new_weights.at[s, :, cols], sems.at[0, side, i]),
            pltpu.make_async_copy(mom.at[i, :, cols], new_bank.at[chosen[0, s], :, cols], sems.at[1, side, i]),
        )

    def fill(n, j):
        for side, ref, i, s, cols in blocks(n, j):
            flag = residual_weight * refresh[s].astype(f32)
            both = halves(basis[s])
            ortho = ref[pl.ds(j * ROWS, ROWS)].astype(f32)
            value = weights[s, :, cols].astype(f32) * (1.0 - step_rate * decay_rate) - scale_step * ortho
            updated[i, :, cols] = value.astype(bf16)
            proj = ref[pl.ds(SIDE * ROWS + j * RANK, RANK)]
            proj = ((1.0 - flag) * proj.astype(f32)).astype(bf16)
            low = mm_t(both, jnp.concatenate([proj, proj], axis=0))
            value = momentum_decay * bank[chosen[0, s], :, cols].astype(f32) + (
                flag * grads[s, :, cols].astype(f32) + low
            )
            mom[i, :, cols] = value.astype(bf16)
            for copy in copies(side, i, s, cols):
                copy.start()

    for n in range(len(parts)):
        if unroll:
            for j in range(SIDE):
                fill(n, j)
        else:

            @pl.loop(0, SIDE // 2)
            def _(j):
                fill(n, 2 * j)
                fill(n, 2 * j + 1)

    for n in range(len(parts)):

        @pl.loop(0, SIDE)
        def _(j):
            for side, _, i, s, cols in blocks(n, j):
                for copy in copies(side, i, s, cols):
                    copy.wait()


def finish(parts, unroll, chosen, refresh, grads, bank, basis, weights, got, into):
    pieces = []
    for chunk, k in parts:
        pieces += [got[chunk][0][k], got[chunk][1][k]]
    count = len(pieces) + len(into)
    return list(
        call(
            functools.partial(finish_kernel, parts, unroll, count),
            [shape(CHUNKS * PER_CHUNK, ROWS, FF)] * 2,
            [SMEM] * 2 + [VMEM] * (4 + len(pieces)) + [HBM] * len(into),
            [HBM] * 2,
            [
                pltpu.VMEM((SIDE * len(parts), ROWS, FF), bf16),
                pltpu.VMEM((SIDE * len(parts), ROWS, FF), bf16),
                pltpu.SemaphoreType.DMA((2, 2, SIDE * len(parts))),
            ],
            30,
            1.5e8 * len(parts),
            2.5e6 * len(parts),
            {6 + len(pieces) + k: k for k in range(len(into))},
        )(chosen, refresh, grads, bank, basis, weights, *pieces, *into)
    )


def send(array, dx, dz):
    pairs = [
        (x * SIDE + z, ((x + dx) % SIDE) * SIDE + (z + dz) % SIDE)
        for x in range(SIDE)
        for z in range(SIDE)
    ]
    return lax.ppermute(array, "row", pairs)


STARTS = (("x", 2), ("z", 2), ("x", 1), ("z", 1), ("x", 3), ("z", 3))


def exchange(over_x, over_z, sign):
    got_x, got_z = [over_x[0], None, None, None], [over_z[0], None, None, None]
    for axis, k in STARTS:
        if axis == "x":
            got_x[k] = send(over_x[k], sign * k, 0)
        else:
            got_z[k] = send(over_z[k], 0, sign * k)
    return got_x, got_z


def step(sampled, refresh, bank, weights, grads, basis):
    basis_t = jnp.swapaxes(basis, 1, 2)
    state = (sampled, refresh, grads, bank, basis_t)
    kept = tuple(pltpu.with_memory_space_constraint(value, pltpu.HBM) for value in state)

    got = []
    left, right = pack(0, (2,), *kept)
    more_left, more_right = pack(0, (1, 3, 0), *state)
    got.append(exchange({**left, **more_left}, {**right, **more_right}, 1))
    left, right = pack(1, (2, 1, 3, 0), *state)
    got.append(exchange(left, right, 1))
    arrived = []
    for chunk in range(2):
        got_x, got_z = got[chunk]
        mixed = mix(got_x + got_z)
        got_x, got_z = exchange(mixed[SIDE:], mixed[:SIDE], 1)
        arrived.append(got_z + got_x)
    backs = [orthogonalize(0, refresh, arrived[0])]
    arrived[1], _ = lax.optimization_barrier((arrived[1], backs[0][0]))
    backs.append(orthogonalize(1, refresh, arrived[1]))
    last = []
    for chunk in range(2):
        back = backs[chunk]
        got_x, got_z = exchange(back[SIDE:], back[:SIDE], -1)
        turned = turn(got_z + got_x)
        last.append(exchange(turned[:SIDE], turned[SIDE:], -1))
    outs = finish(((0, 0), (0, 2)), False, *state, weights, last, [])
    outs = finish(((0, 1), (0, 3), (1, 0), (1, 2)), True, *state, weights, last, outs)
    outs = finish(((1, 1), (1, 3)), True, *state, weights, last, outs)
    return tuple(outs)


def solution(mesh):
    in_specs = (
        P("expert", None),
        P("expert"),
        P("expert", "row", None),
        P("expert", "row", None),
        P("expert", "row", None),
        P("expert", "row", None),
    )
    out_specs = (P("expert", "row", None), P("expert", "row", None))
    return jax.shard_map(step, mesh=mesh, in_specs=in_specs, out_specs=out_specs, check_vma=False)
```

```python
import functools
import math

import jax
import jax.numpy as jnp
from jax import lax
from jax.experimental import pallas as pl
from jax.experimental.pallas import tpu as pltpu
from jax.sharding import PartitionSpec as P


D = 2048
FF = 512
HALF = 256
RANK = 64
ROWS = 128
SIDE = 4
PER_CHUNK = 16
CHUNKS = 2
PACK = ROWS + 16
FULL = PACK + RANK
MIX = SIDE * PACK + RANK
BACK = SIDE * ROWS + RANK
LAST = SIDE * ROWS + SIDE * RANK

momentum_decay = 0.9
residual_weight = 2.0
step_rate = 0.5
decay_rate = 0.1
coef_first = 3.4445
coef_second = -4.775
coef_third = 2.0315
epsilon = 1e-07


SMEM = pl.BlockSpec(memory_space=pltpu.SMEM)
VMEM = pl.BlockSpec(memory_space=pltpu.VMEM)
HBM = pl.BlockSpec(memory_space=pltpu.HBM)
bf16 = jnp.bfloat16
f32 = jnp.float32


def shape(*dims, dtype=bf16):
    return jax.ShapeDtypeStruct(dims, dtype)


def call(kernel, out_shape, in_specs, out_specs, scratch, limit, flops, moved, aliases=None):
    return pl.pallas_call(
        kernel,
        out_shape=out_shape,
        in_specs=in_specs,
        out_specs=out_specs,
        scratch_shapes=scratch,
        input_output_aliases=aliases or {},
        compiler_params=pltpu.CompilerParams(vmem_limit_bytes=limit << 20),
        cost_estimate=pl.CostEstimate(flops=int(flops), bytes_accessed=int(moved), transcendentals=0),
    )


def position():
    me = lax.axis_index("row")
    return lax.div(me, SIDE), lax.rem(me, SIDE)


def plus(place, dx, dz):
    return lax.rem(place[0] + dx, SIDE) * SIDE + lax.rem(place[1] + dz, SIDE)


def mm(a, b):
    return jnp.dot(a, b, preferred_element_type=f32)


def mm_t(a, b):
    return lax.dot_general(a, b, (((0,), (0,)), ((), ())), preferred_element_type=f32)


def halves(value):
    high = value.astype(bf16)
    return jnp.concatenate([high, (value - high.astype(f32)).astype(bf16)], axis=0)


def added(parts):
    total = parts[0].astype(f32)
    for part in parts[1:]:
        total = total + part.astype(f32)
    return total.astype(bf16)


def pack_kernel(chunk, steps, chosen_in, refresh_in, grads, bank, basis, *rest):
    left, right = rest[: len(steps)], rest[len(steps) : 2 * len(steps)]
    g, old, bt, chosen, refresh, sems, flags = rest[2 * len(steps) :]
    place = position()
    base = chunk * PER_CHUNK
    small = (
        pltpu.make_async_copy(chosen_in, chosen, flags.at[0]),
        pltpu.make_async_copy(refresh_in, refresh, flags.at[1]),
    )
    for copy in small:
        copy.start()

    jobs = []
    for n, k in enumerate(steps):
        for j in range(SIDE):
            jobs.append((k * SIDE + j, 0, left[n], j))
            jobs.append((j * SIDE + k, 1, right[n], j))

    def number(i):
        return base + plus(place, i // SIDE, i % SIDE)

    def columns(side):
        return slice(side * HALF, (side + 1) * HALF)

    basis_copies = {}
    block_copies = []
    for i, side, _, _ in jobs:
        if i not in basis_copies:
            basis_copies[i] = pltpu.make_async_copy(basis.at[number(i)], bt.at[i], sems.at[2, 0, i])
            basis_copies[i].start()
        copy = pltpu.make_async_copy(
            grads.at[number(i), :, columns(side)], g.at[i, :, columns(side)], sems.at[0, side, i]
        )
        copy.start()
        block_copies.append([copy])
    for copy in small:
        copy.wait()
    for (i, side, _, _), copies in zip(jobs, block_copies):
        copy = pltpu.make_async_copy(
            bank.at[chosen[0, number(i)], :, columns(side)], old.at[i, :, columns(side)], sems.at[1, side, i]
        )
        copy.start()
        copies.append(copy)

    ready = set()
    for n, (i, side, out, at) in enumerate(jobs):
        if n % 8 == 0:
            for (later, _, _, _), copies in zip(jobs[n : n + 8], block_copies[n : n + 8]):
                for copy in copies:
                    copy.wait()
                if later not in ready:
                    basis_copies[later].wait()
                    ready.add(later)
        flag = residual_weight * refresh[number(i)].astype(f32)
        both = halves(bt[i])
        grad = g[i, :, columns(side)]
        value = momentum_decay * old[i, :, columns(side)].astype(f32) + flag * grad.astype(f32)
        at = at * FULL
        out[at : at + ROWS] = value.astype(bf16)
        first = 32 * side
        out[at + ROWS : at + PACK, :128] = both[first : first + 16]
        out[at + ROWS : at + PACK, 128:] = both[first + 16 : first + 32]
        part = mm(both, grad)
        out[at + PACK : at + FULL] = (part[:RANK] + part[RANK:]).astype(bf16)


def pack(chunk, steps, chosen, refresh, grads, bank, basis):
    outs = call(
        functools.partial(pack_kernel, chunk, steps),
        [shape(SIDE * FULL, HALF)] * (2 * len(steps)),
        [HBM] * 5,
        [VMEM] * (2 * len(steps)),
        [
            pltpu.VMEM((PER_CHUNK, ROWS, FF), bf16),
            pltpu.VMEM((PER_CHUNK, ROWS, FF), bf16),
            pltpu.VMEM((PER_CHUNK, RANK, ROWS), f32),
            pltpu.SMEM((1, CHUNKS * PER_CHUNK), jnp.int32),
            pltpu.SMEM((CHUNKS * PER_CHUNK,), jnp.int32),
            pltpu.SemaphoreType.DMA((3, 2, PER_CHUNK)),
            pltpu.SemaphoreType.DMA((2,)),
        ],
        22,
        1e8 * len(steps),
        3e6 * len(steps),
    )(chosen, refresh, grads, bank, basis)
    return dict(zip(steps, outs[: len(steps)])), dict(zip(steps, outs[len(steps) :]))


def mix_kernel(*refs):
    outs = refs[2 * SIDE :]
    for side in range(2):
        got = refs[side * SIDE : (side + 1) * SIDE]
        out = outs[side * SIDE : (side + 1) * SIDE]
        for to in range(SIDE):
            at = to * FULL
            for src in range(SIDE):
                out[to][src * PACK : (src + 1) * PACK] = got[src][at : at + PACK]
            out[to][SIDE * PACK : MIX] = added([ref[at + PACK : at + FULL] for ref in got])


def mix(got):
    return call(
        mix_kernel,
        [shape(MIX, HALF)] * (2 * SIDE),
        [VMEM] * (2 * SIDE),
        [VMEM] * (2 * SIDE),
        [],
        16,
        1e6,
        6e6,
    )(*got)


def ortho_kernel(chunk, refresh, *refs):
    q_left, q_right = refs[:SIDE], refs[SIDE : 2 * SIDE]
    b_left, b_right = refs[2 * SIDE : 3 * SIDE], refs[3 * SIDE : 4 * SIDE]
    m, acc, gram, f_one, f_two, work = refs[4 * SIDE :]
    place = position()
    keep = 1.0 - residual_weight * refresh[chunk * PER_CHUNK + plus(place, 0, 0)].astype(f32)
    proj = [added([ref[SIDE * PACK : MIX] for ref in q]) for q in (q_left, q_right)]
    near = (keep * jnp.concatenate(proj, axis=1).astype(f32)).astype(bf16)
    for k in range(SIDE):
        b_left[k][SIDE * ROWS : BACK] = proj[0]
        b_right[k][SIDE * ROWS : BACK] = proj[1]

    for i in range(PER_CHUNK):
        dx, dz = i // SIDE, i % SIDE
        pieces = []
        for ref, at in ((q_left[dz], dx * PACK), (q_right[dx], dz * PACK)):
            pieces += [ref[at + ROWS : at + PACK, :128], ref[at + ROWS : at + PACK, 128:]]
        low = mm_t(jnp.concatenate(pieces, axis=0), near)
        for side, ref, at in ((0, q_left[dz], dx * PACK), (1, q_right[dx], dz * PACK)):
            cols = slice(side * HALF, (side + 1) * HALF)
            m[i * ROWS : (i + 1) * ROWS, cols] = (ref[at : at + ROWS].astype(f32) + low[:, cols]).astype(bf16)

    acc[...] = mm_t(m[:1024], m[:1024])
    acc[...] += mm_t(m[1024:], m[1024:])

    tile = (ROWS, ROWS)
    diagonal = lax.broadcasted_iota(jnp.int32, tile, 0) == lax.broadcasted_iota(jnp.int32, tile, 1)
    blocks = [slice(k * ROWS, (k + 1) * ROWS) for k in range(FF // ROWS)]
    trace = jnp.zeros(tile, f32)
    for block in blocks:
        trace += jnp.where(diagonal, acc[block, block], 0.0)
    inverse = 1.0 / (jnp.sqrt(jnp.sum(trace, axis=(0, 1), keepdims=True)) + epsilon)
    for block in blocks:
        gram[block, :] = (acc[block, :] * (inverse * inverse)).astype(bf16)

    def factor(out):
        for at in range(0, FF, HALF):
            rows = slice(at, at + HALF)
            part = gram[rows, :]
            value = coef_second * part.astype(f32) + coef_third * mm(part, gram[...])
            out[rows, :] = value.astype(bf16)
        for block in blocks:
            part = out[block, block].astype(f32)
            out[block, block] = jnp.where(diagonal, part + coef_first, part).astype(bf16)

    def advance(factor_ref):
        work[...] = mm(gram[...], factor_ref[...]).astype(bf16)
        gram[...] = mm(work[...], factor_ref[...]).astype(bf16)

    factor(f_one)
    advance(f_one)
    factor(f_two)
    advance(f_two)
    work[...] = mm(f_one[...], f_two[...]).astype(bf16)
    factor(f_one)
    f_two[...] = (inverse * mm(work[...], f_one[...])).astype(bf16)

    for side in (0, 1):
        right = f_two[:, side * HALF : (side + 1) * HALF]
        for dx in range(SIDE):
            value = mm(m[dx * 512 : (dx + 1) * 512, :], right).astype(bf16)
            for dz in range(SIDE):
                piece = value[dz * ROWS : (dz + 1) * ROWS]
                if side == 0:
                    b_left[dz][dx * ROWS : (dx + 1) * ROWS] = piece
                else:
                    b_right[dx][dz * ROWS : (dz + 1) * ROWS] = piece


def orthogonalize(chunk, refresh, got):
    return call(
        functools.partial(ortho_kernel, chunk),
        [shape(BACK, HALF)] * (2 * SIDE),
        [SMEM] + [VMEM] * (2 * SIDE),
        [VMEM] * (2 * SIDE),
        [
            pltpu.VMEM((D, FF), bf16),
            pltpu.VMEM((FF, FF), f32),
            pltpu.VMEM((FF, FF), bf16),
            pltpu.VMEM((FF, FF), bf16),
            pltpu.VMEM((FF, FF), bf16),
            pltpu.VMEM((FF, FF), bf16),
        ],
        28,
        8e9,
        5e6,
    )(refresh, *got)


def turn_kernel(*refs):
    outs = refs[2 * SIDE :]
    for side in range(2):
        got = refs[side * SIDE : (side + 1) * SIDE]
        out = outs[side * SIDE : (side + 1) * SIDE]
        for to in range(SIDE):
            for src in range(SIDE):
                out[to][src * ROWS : (src + 1) * ROWS] = got[src][to * ROWS : (to + 1) * ROWS]
                at = SIDE * ROWS + src * RANK
                out[to][at : at + RANK] = got[src][SIDE * ROWS : BACK]


def turn(got):
    return call(
        turn_kernel,
        [shape(LAST, HALF)] * (2 * SIDE),
        [VMEM] * (2 * SIDE),
        [VMEM] * (2 * SIDE),
        [],
        16,
        1e3,
        4e6,
    )(*got)


def finish_kernel(parts, unroll, count, chosen, refresh, grads, bank, basis, weights, *refs):
    new_bank, new_weights, mom, updated, sems = refs[count:]
    place = position()
    scale_step = step_rate * 0.2 * math.sqrt(max(D, FF))

    def blocks(n, j):
        chunk, k = parts[n]
        for side, dx, dz in ((0, k, j), (1, j, k)):
            s = chunk * PER_CHUNK + plus(place, dx, dz)
            yield side, refs[2 * n + side], n * SIDE + j, s, slice(side * HALF, (side + 1) * HALF)

    def copies(side, i, s, cols):
        return (
            pltpu.make_async_copy(updated.at[i, :, cols], new_weights.at[s, :, cols], sems.at[0, side, i]),
            pltpu.make_async_copy(mom.at[i, :, cols], new_bank.at[chosen[0, s], :, cols], sems.at[1, side, i]),
        )

    def fill(n, j):
        for side, ref, i, s, cols in blocks(n, j):
            flag = residual_weight * refresh[s].astype(f32)
            both = halves(basis[s])
            ortho = ref[pl.ds(j * ROWS, ROWS)].astype(f32)
            value = weights[s, :, cols].astype(f32) * (1.0 - step_rate * decay_rate) - scale_step * ortho
            updated[i, :, cols] = value.astype(bf16)
            proj = ref[pl.ds(SIDE * ROWS + j * RANK, RANK)]
            proj = ((1.0 - flag) * proj.astype(f32)).astype(bf16)
            low = mm_t(both, jnp.concatenate([proj, proj], axis=0))
            value = momentum_decay * bank[chosen[0, s], :, cols].astype(f32) + (
                flag * grads[s, :, cols].astype(f32) + low
            )
            mom[i, :, cols] = value.astype(bf16)
            for copy in copies(side, i, s, cols):
                copy.start()

    for n in range(len(parts)):
        if unroll:
            for j in range(SIDE):
                fill(n, j)
        else:

            @pl.loop(0, SIDE // 2)
            def _(j):
                fill(n, 2 * j)
                fill(n, 2 * j + 1)

    for n in range(len(parts)):

        @pl.loop(0, SIDE)
        def _(j):
            for side, _, i, s, cols in blocks(n, j):
                for copy in copies(side, i, s, cols):
                    copy.wait()


def finish(parts, unroll, chosen, refresh, grads, bank, basis, weights, got, into):
    pieces = []
    for chunk, k in parts:
        pieces += [got[chunk][0][k], got[chunk][1][k]]
    count = len(pieces) + len(into)
    return list(
        call(
            functools.partial(finish_kernel, parts, unroll, count),
            [shape(CHUNKS * PER_CHUNK, ROWS, FF)] * 2,
            [SMEM] * 2 + [VMEM] * (4 + len(pieces)) + [HBM] * len(into),
            [HBM] * 2,
            [
                pltpu.VMEM((SIDE * len(parts), ROWS, FF), bf16),
                pltpu.VMEM((SIDE * len(parts), ROWS, FF), bf16),
                pltpu.SemaphoreType.DMA((2, 2, SIDE * len(parts))),
            ],
            30,
            1.5e8 * len(parts),
            2.5e6 * len(parts),
            {6 + len(pieces) + k: k for k in range(len(into))},
        )(chosen, refresh, grads, bank, basis, weights, *pieces, *into)
    )


def send(array, dx, dz):
    pairs = [
        (x * SIDE + z, ((x + dx) % SIDE) * SIDE + (z + dz) % SIDE)
        for x in range(SIDE)
        for z in range(SIDE)
    ]
    return lax.ppermute(array, "row", pairs)


STARTS = (("x", 2), ("z", 2), ("x", 1), ("z", 1), ("x", 3), ("z", 3))


def exchange(over_x, over_z, sign):
    got_x, got_z = [over_x[0], None, None, None], [over_z[0], None, None, None]
    for axis, k in STARTS:
        if axis == "x":
            got_x[k] = send(over_x[k], sign * k, 0)
        else:
            got_z[k] = send(over_z[k], 0, sign * k)
    return got_x, got_z


def step(sampled, refresh, bank, weights, grads, basis):
    basis_t = jnp.swapaxes(basis, 1, 2)
    state = (sampled, refresh, grads, bank, basis_t)
    kept = tuple(pltpu.with_memory_space_constraint(value, pltpu.HBM) for value in state)

    got = []
    left, right = pack(0, (2,), *kept)
    more_left, more_right = pack(0, (1, 3, 0), *state)
    got.append(exchange({**left, **more_left}, {**right, **more_right}, 1))
    left, right = pack(1, (2, 1, 3, 0), *state)
    got.append(exchange(left, right, 1))
    arrived = []
    for chunk in range(2):
        got_x, got_z = got[chunk]
        mixed = mix(got_x + got_z)
        got_x, got_z = exchange(mixed[SIDE:], mixed[:SIDE], 1)
        arrived.append(got_z + got_x)
    backs = [orthogonalize(0, refresh, arrived[0])]
    arrived[1], _ = lax.optimization_barrier((arrived[1], backs[0][0]))
    backs.append(orthogonalize(1, refresh, arrived[1]))
    last = []
    for chunk in range(2):
        back = backs[chunk]
        got_x, got_z = exchange(back[SIDE:], back[:SIDE], -1)
        turned = turn(got_z + got_x)
        last.append(exchange(turned[:SIDE], turned[SIDE:], -1))
    outs = finish(((0, 0), (0, 2)), False, *state, weights, last, [])
    outs = finish(((0, 1), (0, 3), (1, 0), (1, 2), (1, 1)), True, *state, weights, last, outs)
    outs = finish(((1, 3),), True, *state, weights, last, outs)
    return tuple(outs)


def solution(mesh):
    in_specs = (
        P("expert", None),
        P("expert"),
        P("expert", "row", None),
        P("expert", "row", None),
        P("expert", "row", None),
        P("expert", "row", None),
    )
    out_specs = (P("expert", "row", None), P("expert", "row", None))
    return jax.shard_map(step, mesh=mesh, in_specs=in_specs, out_specs=out_specs, check_vma=False)
```
